32 devices in a mesh: tok: 8 (over z, x), head: 4 (over y, core).
Axes of the slice: x: 2, y: 2, z: 4, core: 2. Of those that a mesh axis runs over, the one named last changes fastest.
Arguments:
- queries: bfloat16 [2048, 8192], P(('tok', 'head')), may hold values from -6 to 6
- keys: bfloat16 [2048, 1024], P(('tok', 'head')), may hold values from -6 to 6
- values: bfloat16 [2048, 1024], P(('tok', 'head')), may hold values from -6 to 6
- doc_ids: int32 [2048], replicated, may hold values from 0 to 2, never falling along the last dimension, each value on 1 to 1792 neighbouring positions
Outputs:
- attention: bfloat16 [2048, 8192], P('tok', 'head')
The draws below stay inside these ranges and needn't reach their ends.
Inputs may be any that keep to these rules, and one draw needn't show every extreme that they name: doc_ids never falls along the tokens; each document holds 1 to 1792 tokens and some document holds exactly 1792.
All inputs are finite; a program needn't handle non-finite values.
Results may differ from the reference program's by a relative error of at most 0.0038.
Values may be sent and summed in bfloat16 or wider, within the bound.
A program may use at most 64 MiB of HBM per device.

```python
import math
import jax
import jax.numpy as jnp
import numpy as np
from jax import lax

QH = 64
KVH = 8
HD = 128
TOK_DEV = 256
REACH = 7
TOKENS = 2048
DOC_MAX = 1792
DOCS = 3


def draw_queries(key, part):
    base = jax.random.truncated_normal(jax.random.fold_in(key, 1), -6.0, 6.0, (TOKENS, QH * HD), jnp.float32)
    return base.astype(jnp.bfloat16)


def draw_keys(key, part):
    base = jax.random.truncated_normal(jax.random.fold_in(key, 2), -6.0, 6.0, (TOKENS, KVH * HD), jnp.float32)
    return base.astype(jnp.bfloat16)


def steps_of(own_key, dims, pieces, low, top_value):
    level, own = 1.0, jax.random.fold_in(own_key, 6)
    for position, blocks in pieces:
        heights = jnp.exp(jax.random.uniform(jax.random.fold_in(own, position), (blocks,), jnp.float32, low / len(pieces), top_value / len(pieces)))
        level = level * jnp.repeat(heights, dims[position] // blocks).reshape([-1 if axis == position else 1 for axis in range(len(dims))])
    return level


def split_up(number_of, total, limit, skew):
    loads = [(1 << 20) // math.isqrt(rank ** skew) + 1 for rank in range(2, number_of + 1)]
    spare, given = total - limit - (number_of - 1), [1] * (number_of - 1)
    while spare > 0:
        candidates = [i for i in range(number_of - 1) if given[i] < limit]
        pool, left = sum([loads[i] for i in candidates]), spare
        for i in candidates:
            addition = min(limit - given[i], max(1, left * loads[i] // pool), spare)
            given[i] = given[i] + addition
            spare = spare - addition
    return np.array([limit] + given)


def uneven_parts(stream_key, count, total, most, lean):
    if count == 2:
        one = jax.random.randint(stream_key, (), max(1, total - most), min(most, total - 1) + 1)
        return jnp.stack([one, total - one])
    tallies = jnp.asarray(split_up(count, total, most, lean), jnp.int32)
    twos = (count - 1) // 2
    source_of, sink = tallies[1:1 + 2 * twos:2], tallies[2:2 + 2 * twos:2]
    room = jnp.minimum(source_of - 1, most - sink)
    shifted = jax.random.randint(jax.random.fold_in(stream_key, 1), (twos,), 0, 1 << 20) % (room + 1)
    tallies = tallies.at[1:1 + 2 * twos:2].set(source_of - shifted).at[2:2 + 2 * twos:2].set(sink + shifted)
    return tallies[jax.random.permutation(jax.random.fold_in(stream_key, 2), count)]


def bell_draw(rng, dims, scale, reach, split=(), kind=jnp.bfloat16):
    values = scale * jax.random.normal(rng, dims, jnp.float32)
    if split:
        values = values * steps_of(rng, dims, split, -0.22, 0.18)
    return jnp.clip(values, -reach, reach).astype(kind)


def setup_inputs(seed: int = 0) -> dict:
    arg_keys = jax.random.split(jax.random.key(seed), 5)
    return {
        "queries": draw_queries(jax.random.fold_in(arg_keys[4], 71), 0),
        "keys": draw_keys(jax.random.fold_in(arg_keys[4], 71), 0),
        "values": bell_draw(arg_keys[2], (TOKENS, KVH * HD), 1.0, 6.0, ((0, 32),)),
        "doc_ids": jnp.searchsorted(jnp.cumsum(uneven_parts(arg_keys[3], DOCS, TOKENS, DOC_MAX, 2)), jnp.arange(TOKENS), side="right").astype(jnp.int32),
    }


def reference(queries, keys, values, doc_ids):
    groups = QH // KVH
    extent = REACH * TOK_DEV
    window = extent + TOK_DEV
    scaling = HD ** -0.5
    key_pad = jnp.concatenate([jnp.zeros((extent, KVH * HD), keys.dtype), keys], axis=0)
    value_pad = jnp.concatenate([jnp.zeros((extent, KVH * HD), values.dtype), values], axis=0)
    id_pad = jnp.concatenate([jnp.full((extent,), -1, jnp.int32), doc_ids.astype(jnp.int32)], axis=0)
    lagged = jnp.arange(window, dtype=jnp.int32)[None, :] - extent
    ahead = jnp.arange(TOK_DEV, dtype=jnp.int32)[:, None]
    causal = lagged <= ahead

    def one_block(block_index):
        start = (block_index * TOK_DEV).astype(jnp.int32)
        query_block = lax.dynamic_slice_in_dim(queries, start, TOK_DEV, 0).astype(jnp.float32).reshape(TOK_DEV, KVH, groups, HD)
        key_block = lax.dynamic_slice_in_dim(key_pad, start, window, 0).astype(jnp.float32).reshape(window, KVH, HD)
        value_block = lax.dynamic_slice_in_dim(value_pad, start, window, 0).astype(jnp.float32).reshape(window, KVH, HD)
        query_ids = lax.dynamic_slice_in_dim(doc_ids.astype(jnp.int32), start, TOK_DEV, 0)
        key_ids = lax.dynamic_slice_in_dim(id_pad, start, window, 0)
        visible = (query_ids[:, None] == key_ids[None, :]) & causal
        scores = jnp.einsum("qcgd,kcd->qcgk", query_block, key_block, precision=lax.Precision.HIGHEST) * scaling
        scores = jnp.where(visible[:, None, None, :], scores, -jnp.inf)
        peak = jnp.max(scores, axis=-1, keepdims=True)
        weights = jnp.exp(scores - peak)
        total = jnp.sum(weights, axis=-1)
        rounded = lax.optimization_barrier(weights.astype(jnp.bfloat16))
        numerator = jnp.einsum("qcgk,kcd->qcgd", rounded.astype(jnp.float32), value_block, precision=lax.Precision.HIGHEST)
        return (numerator / total[..., None]).reshape(TOK_DEV, QH * HD).astype(jnp.bfloat16)

    blocks = lax.map(one_block, jnp.arange(TOKENS // TOK_DEV, dtype=jnp.int32))
    return blocks.reshape(TOKENS, QH * HD)
```

```python
import functools

import jax
import jax.numpy as jnp
from jax import lax
from jax.experimental import pallas as pl
from jax.experimental.pallas import tpu as pltpu
from jax.sharding import PartitionSpec as P

QH = 64
KVH = 8
HD = 128
REACH = 7
GROUPS = QH // KVH
MESH = pl.DeviceIdType.MESH
NEG = -1e30
SCALE = HD ** -0.5 * 1.4426950408889634
ROWS = 128


def kernel(
    tok_len, head_len, hops,
    q_hbm, k_hbm, v_hbm, ids_ref, out_ref,
    q_buf, kv, bias, peak, part, acc,
    own_sem, kv_send, kv_recv, q_send, q_recv, z_send, z_recv, x_send, x_recv,
):
    t, h = lax.axis_index("tok"), lax.axis_index("head")
    level, parity = t // 2, lax.rem(t, 2)
    partner = level * 2 + (1 - parity)
    levels = tok_len // 2
    piece = q_hbm.shape[0]
    kv_heads, shard, wide = q_buf.shape
    q_cols, kv_cols = kv_heads * wide, kv_heads * HD

    barrier = pltpu.get_barrier_semaphore()
    greeted = head_len
    for d in range(1, head_len):
        pl.semaphore_signal(
            barrier, inc=1, device_id={"tok": t, "head": lax.rem(h + d, head_len)}, device_id_type=MESH
        )
    pl.semaphore_signal(barrier, inc=1, device_id={"tok": partner, "head": h}, device_id_type=MESH)
    for k in range(1, hops + 1):
        @pl.when(level + k < levels)
        def _():
            pl.semaphore_signal(barrier, inc=1, device_id={"tok": t + 2 * k, "head": h}, device_id_type=MESH)

        @pl.when(level - k >= 0)
        def _():
            pl.semaphore_signal(barrier, inc=1, device_id={"tok": t - 2 * k, "head": h}, device_id_type=MESH)
    greeted = greeted + jnp.minimum(levels - 1 - level, hops) + jnp.minimum(level, hops)
    pl.semaphore_wait(barrier, greeted)

    rows = pl.ds(pl.multiple_of(h * piece, piece), piece)

    def kv_piece(d, which, source):
        g = lax.rem(h + d, head_len)
        return pltpu.make_async_remote_copy(
            src_ref=source.at[:, pl.ds(pl.multiple_of(g * kv_cols, kv_cols), kv_cols)],
            dst_ref=kv.at[0, parity, which, rows, :],
            send_sem=kv_send.at[d, which],
            recv_sem=kv_recv.at[d, which],
            device_id={"tok": t, "head": g},
            device_id_type=MESH,
        )

    def q_piece(d, c):
        g = lax.rem(h + d, head_len)
        return pltpu.make_async_remote_copy(
            src_ref=q_hbm.at[:, pl.ds(pl.multiple_of(g * q_cols + c * wide, wide), wide)],
            dst_ref=q_buf.at[c, rows, :],
            send_sem=q_send.at[d, c],
            recv_sem=q_recv.at[d, c],
            device_id={"tok": t, "head": g},
            device_id_type=MESH,
        )

    def own_kv(which, source):
        return pltpu.make_async_copy(
            source.at[:, pl.ds(pl.multiple_of(h * kv_cols, kv_cols), kv_cols)],
            kv.at[0, parity, which, rows, :],
            own_sem.at[which],
        )

    def own_q(c):
        return pltpu.make_async_copy(
            q_hbm.at[:, pl.ds(pl.multiple_of(h * q_cols + c * wide, wide), wide)],
            q_buf.at[c, rows, :],
            own_sem.at[2 + c],
        )

    def push(k):
        return pltpu.make_async_remote_copy(
            src_ref=kv.at[0, parity],
            dst_ref=kv.at[k, parity],
            send_sem=z_send.at[k],
            recv_sem=z_recv.at[k],
            device_id={"tok": t + 2 * k, "head": h},
            device_id_type=MESH,
        )

    def share(k):
        return pltpu.make_async_remote_copy(
            src_ref=kv.at[k, parity],
            dst_ref=kv.at[k, parity],
            send_sem=x_send.at[k],
            recv_sem=x_recv.at[k],
            device_id={"tok": partner, "head": h},
            device_id_type=MESH,
        )

    sources = (k_hbm, v_hbm)
    for d in range(1, head_len):
        for which in range(2):
            kv_piece(d, which, sources[which]).start()
    for which in range(2):
        own_kv(which, sources[which]).start()
    for c in range(kv_heads):
        for d in range(1, head_len):
            q_piece(d, c).start()
        own_q(c).start()

    for which in range(2):
        own_kv(which, sources[which]).wait()
        for d in range(1, head_len):
            kv_piece(d, which, sources[which]).wait_recv()
    share(0).start()
    for k in range(1, hops + 1):
        @pl.when(level + k < levels)
        def _():
            push(k).start()

    own_ids = ids_ref[:, pl.ds(pl.multiple_of(t * shard, shard), shard)]
    column = jnp.broadcast_to(own_ids, (2 * shard, shard)).T
    q_pos = t * shard + lax.broadcasted_iota(jnp.int32, (shard, 2 * shard), 0)
    k_iota = lax.broadcasted_iota(jnp.int32, (shard, 2 * shard), 1)
    for k in range(hops + 1):
        @pl.when(level - k >= 0)
        def _():
            start = (level - k) * 2 * shard
            key_ids = ids_ref[:, pl.ds(pl.multiple_of(start, 2 * shard), 2 * shard)]
            visible = (column == key_ids) & (start + k_iota <= q_pos)
            bias[k] = jnp.where(visible, 0.0, NEG)

    def absorb(k, c, first):
        def head(j, carry):
            lanes = pl.ds(pl.multiple_of(j * HD, HD), HD)
            heads = pl.ds(pl.multiple_of(c * HD, HD), HD)
            index = c * GROUPS + j
            keys = [kv[k, s, 0, :, heads] for s in range(2)]
            vals = [kv[k, s, 1, :, heads] for s in range(2)]
            for r in range(0, shard, ROWS):
                q = q_buf[c, pl.ds(r, ROWS), lanes]
                tiles = []
                for s in range(2):
                    score = lax.dot_general(
                        q, keys[s], (((1,), (1,)), ((), ())), preferred_element_type=jnp.float32
                    )
                    score = score * SCALE + bias[k, pl.ds(r, ROWS), s * shard:(s + 1) * shard]
                    tiles += [score[:, i:i + HD] for i in range(0, shard, HD)]
                top = functools.reduce(jnp.maximum, tiles)
                top = jnp.broadcast_to(jnp.max(top, axis=1, keepdims=True), (ROWS, HD))
                if not first:
                    before = peak[index, pl.ds(r, ROWS), :]
                    top = jnp.maximum(before, top)
                    decay = jnp.exp2(before - top)
                peak[index, pl.ds(r, ROWS), :] = top
                weights = [jnp.exp2(tile - top) for tile in tiles]
                total = functools.reduce(jnp.add, weights)
                rounded = [w.astype(jnp.bfloat16) for w in weights]
                half = len(rounded) // 2
                update = jnp.dot(
                    jnp.concatenate(rounded[:half], axis=1), vals[0], preferred_element_type=jnp.float32
                ) + jnp.dot(
                    jnp.concatenate(rounded[half:], axis=1), vals[1], preferred_element_type=jnp.float32
                )
                if not first:
                    total = part[index, pl.ds(r, ROWS), :] * decay + total
                    update = acc[index, pl.ds(r, ROWS), :] * decay + update
                part[index, pl.ds(r, ROWS), :] = total
                acc[index, pl.ds(r, ROWS), :] = update
            return carry

        lax.fori_loop(0, GROUPS, head, 0, unroll=2)

    def relay(k):
        if k <= hops:
            @pl.when(level - k >= 0)
            def _():
                push(k).wait_recv()
                share(k).start()

    relay(1)
    share(0).wait_recv()
    for c in range(kv_heads):
        own_q(c).wait()
        for d in range(1, head_len):
            q_piece(d, c).wait_recv()

        absorb(0, c, True)
    for k in range(1, hops + 1):
        relay(k + 1)

        @pl.when(level - k >= 0)
        def _():
            share(k).wait_recv()

            def pair(c, carry):
                absorb(k, c, False)
                return carry

            lax.fori_loop(0, kv_heads, pair, 0)

    def finish(index, carry):
        total = jnp.sum(part[index], axis=1, keepdims=True)
        result = (acc[index] * (1.0 / total)).astype(out_ref.dtype)
        out_ref[:, pl.ds(pl.multiple_of(index * HD, HD), HD)] = result
        return carry

    lax.fori_loop(0, kv_heads * GROUPS, finish, 0, unroll=2)

    for d in range(1, head_len):
        for which in range(2):
            kv_piece(d, which, sources[which]).wait_send()
        for c in range(kv_heads):
            q_piece(d, c).wait_send()
    share(0).wait_send()
    for k in range(1, hops + 1):
        @pl.when(level + k < levels)
        def _():
            push(k).wait_send()

        @pl.when(level - k >= 0)
        def _():
            share(k).wait_send()


def body(queries, keys, values, doc_ids):
    tok_len, head_len = lax.axis_size("tok"), lax.axis_size("head")
    shard = queries.shape[0] * head_len
    kv_heads = KVH // head_len
    wide = GROUPS * HD
    hops = min((REACH + 1) // 2, tok_len // 2 - 1)
    heads = kv_heads * GROUPS
    DMA = pltpu.SemaphoreType.DMA
    anywhere = pl.BlockSpec(memory_space=pl.ANY)
    vmem = pl.BlockSpec(memory_space=pltpu.VMEM)
    return pl.pallas_call(
        functools.partial(kernel, tok_len, head_len, hops),
        out_shape=jax.ShapeDtypeStruct((shard, heads * HD), jnp.bfloat16),
        in_specs=[anywhere, anywhere, anywhere, vmem],
        out_specs=vmem,
        scratch_shapes=[
            pltpu.VMEM((kv_heads, shard, wide), jnp.bfloat16),
            pltpu.VMEM((hops + 1, 2, 2, shard, kv_heads * HD), jnp.bfloat16),
            pltpu.VMEM((hops + 1, shard, 2 * shard), jnp.float32),
            pltpu.VMEM((heads, shard, HD), jnp.float32),
            pltpu.VMEM((heads, shard, HD), jnp.float32),
            pltpu.VMEM((heads, shard, HD), jnp.float32),
            DMA((2 + kv_heads,)),
            DMA((head_len, 2)),
            DMA((head_len, 2)),
            DMA((head_len, kv_heads)),
            DMA((head_len, kv_heads)),
            DMA((hops + 1,)),
            DMA((hops + 1,)),
            DMA((hops + 1,)),
            DMA((hops + 1,)),
        ],
        compiler_params=pltpu.CompilerParams(
            collective_id=0, has_side_effects=True, vmem_limit_bytes=48 * 1024 * 1024
        ),
    )(queries, keys, values, doc_ids.reshape(1, -1))


def solution(mesh):
    return jax.shard_map(
        body,
        mesh=mesh,
        in_specs=(
            P(("tok", "head"), None),
            P(("tok", "head"), None),
            P(("tok", "head"), None),
            P(),
        ),
        out_specs=P("tok", "head"),
        check_vma=False,
    )
```

```python
import functools

import jax
import jax.numpy as jnp
from jax import lax
from jax.experimental import pallas as pl
from jax.experimental.pallas import tpu as pltpu
from jax.sharding import PartitionSpec as P

QH = 64
KVH = 8
HD = 128
REACH = 7
GROUPS = QH // KVH
MESH = pl.DeviceIdType.MESH
NEG = -1e30
SCALE = HD ** -0.5 * 1.4426950408889634
ROWS = 256


def kernel(
    tok_len, head_len, hops,
    q_hbm, k_hbm, v_hbm, ids_ref, out_ref,
    q_buf, kv, bias, peak, part, acc,
    own_sem, kv_send, kv_recv, q_send, q_recv, z_send, z_recv, x_send, x_recv,
):
    t, h = lax.axis_index("tok"), lax.axis_index("head")
    level, parity = t // 2, lax.rem(t, 2)
    partner = level * 2 + (1 - parity)
    levels = tok_len // 2
    piece = q_hbm.shape[0]
    kv_heads, shard, wide = q_buf.shape
    q_cols, kv_cols = kv_heads * wide, kv_heads * HD

    barrier = pltpu.get_barrier_semaphore()
    greeted = head_len
    for d in range(1, head_len):
        pl.semaphore_signal(
            barrier, inc=1, device_id={"tok": t, "head": lax.rem(h + d, head_len)}, device_id_type=MESH
        )
    pl.semaphore_signal(barrier, inc=1, device_id={"tok": partner, "head": h}, device_id_type=MESH)
    for k in range(1, hops + 1):
        @pl.when(level + k < levels)
        def _():
            pl.semaphore_signal(barrier, inc=1, device_id={"tok": t + 2 * k, "head": h}, device_id_type=MESH)

        @pl.when(level - k >= 0)
        def _():
            pl.semaphore_signal(barrier, inc=1, device_id={"tok": t - 2 * k, "head": h}, device_id_type=MESH)
    greeted = greeted + jnp.minimum(levels - 1 - level, hops) + jnp.minimum(level, hops)
    pl.semaphore_wait(barrier, greeted)

    rows = pl.ds(pl.multiple_of(h * piece, piece), piece)

    def kv_piece(d, which, source):
        g = lax.rem(h + d, head_len)
        return pltpu.make_async_remote_copy(
            src_ref=source.at[:, pl.ds(pl.multiple_of(g * kv_cols, kv_cols), kv_cols)],
            dst_ref=kv.at[0, parity, which, rows, :],
            send_sem=kv_send.at[d, which],
            recv_sem=kv_recv.at[d, which],
            device_id={"tok": t, "head": g},
            device_id_type=MESH,
        )

    def q_piece(d, c):
        g = lax.rem(h + d, head_len)
        return pltpu.make_async_remote_copy(
            src_ref=q_hbm.at[:, pl.ds(pl.multiple_of(g * q_cols + c * wide, wide), wide)],
            dst_ref=q_buf.at[c, rows, :],
            send_sem=q_send.at[d, c],
            recv_sem=q_recv.at[d, c],
            device_id={"tok": t, "head": g},
            device_id_type=MESH,
        )

    def own_kv(which, source):
        return pltpu.make_async_copy(
            source.at[:, pl.ds(pl.multiple_of(h * kv_cols, kv_cols), kv_cols)],
            kv.at[0, parity, which, rows, :],
            own_sem.at[which],
        )

    def own_q(c):
        return pltpu.make_async_copy(
            q_hbm.at[:, pl.ds(pl.multiple_of(h * q_cols + c * wide, wide), wide)],
            q_buf.at[c, rows, :],
            own_sem.at[2 + c],
        )

    def push(k, which):
        return pltpu.make_async_remote_copy(
            src_ref=kv.at[0, parity, which],
            dst_ref=kv.at[k, parity, which],
            send_sem=z_send.at[k, which],
            recv_sem=z_recv.at[k, which],
            device_id={"tok": t + 2 * k, "head": h},
            device_id_type=MESH,
        )

    def share(k, which):
        return pltpu.make_async_remote_copy(
            src_ref=kv.at[k, parity, which],
            dst_ref=kv.at[k, parity, which],
            send_sem=x_send.at[k, which],
            recv_sem=x_recv.at[k, which],
            device_id={"tok": partner, "head": h},
            device_id_type=MESH,
        )

    sources = (k_hbm, v_hbm)
    for d in range(1, head_len):
        for which in range(2):
            kv_piece(d, which, sources[which]).start()
    for which in range(2):
        own_kv(which, sources[which]).start()
    for which in range(2):
        own_kv(which, sources[which]).wait()
        for d in range(1, head_len):
            kv_piece(d, which, sources[which]).wait_recv()
        share(0, which).start()
        for k in range(1, 2):
            @pl.when(level + k < levels)
            def _():
                push(k, which).start()
    for k in range(2, hops + 1):
        @pl.when(level + k < levels)
        def _():
            for which in range(2):
                push(k, which).start()
    for c in range(kv_heads):
        for d in range(1, head_len):
            q_piece(d, c).start()
        own_q(c).start()

    own_ids = ids_ref[:, pl.ds(pl.multiple_of(t * shard, shard), shard)]
    column = jnp.broadcast_to(own_ids, (2 * shard, shard)).T
    q_pos = t * shard + lax.broadcasted_iota(jnp.int32, (shard, 2 * shard), 0)
    k_iota = lax.broadcasted_iota(jnp.int32, (shard, 2 * shard), 1)
    for k in range(hops + 1):
        @pl.when(level - k >= 0)
        def _():
            start = (level - k) * 2 * shard
            key_ids = ids_ref[:, pl.ds(pl.multiple_of(start, 2 * shard), 2 * shard)]
            visible = (column == key_ids) & (start + k_iota <= q_pos)
            bias[k] = jnp.where(visible, 0.0, NEG)

    def absorb(k, c, shards, first):
        def head(j, carry):
            lanes = pl.ds(pl.multiple_of(j * HD, HD), HD)
            heads = pl.ds(pl.multiple_of(c * HD, HD), HD)
            index = c * GROUPS + j
            keys = [kv[k, s, 0, :, heads] for s in shards]
            vals = [kv[k, s, 1, :, heads] for s in shards]
            q = q_buf[c, :, lanes]
            tiles = []
            for s, key in zip(shards, keys):
                score = lax.dot_general(
                    q, key, (((1,), (1,)), ((), ())), preferred_element_type=jnp.float32
                )
                score = score * SCALE + bias[k, :, pl.ds(pl.multiple_of(s * shard, shard), shard)]
                tiles += [score[:, i:i + HD] for i in range(0, shard, HD)]
            top = functools.reduce(jnp.maximum, tiles)
            top = jnp.broadcast_to(jnp.max(top, axis=1, keepdims=True), (shard, HD))
            if not first:
                before = peak[index]
                top = jnp.maximum(before, top)
                decay = jnp.exp2(before - top)
            peak[index] = top
            weights = [jnp.exp2(tile - top) for tile in tiles]
            total = functools.reduce(jnp.add, weights)
            rounded = [w.astype(jnp.bfloat16) for w in weights]
            step = shard // HD
            update = functools.reduce(jnp.add, [
                jnp.dot(
                    jnp.concatenate(rounded[n * step:(n + 1) * step], axis=1), val,
                    preferred_element_type=jnp.float32,
                )
                for n, val in enumerate(vals)
            ])
            if not first:
                total = part[index] * decay + total
                update = acc[index] * decay + update
            part[index] = total
            acc[index] = update
            return carry

        lax.fori_loop(0, GROUPS, head, 0, unroll=2)

    def relay(k):
        if k <= hops:
            @pl.when(level - k >= 0)
            def _():
                for which in range(2):
                    push(k, which).wait_recv()
                    share(k, which).start()

    def await_share(k):
        for which in range(2):
            share(k, which).wait_recv()

    relay(1)
    await_share(0)
    for c in range(kv_heads):
        own_q(c).wait()
        for d in range(1, head_len):
            q_piece(d, c).wait_recv()
        if c == kv_heads - 1:
            relay(2)
        absorb(0, c, (0, 1), True)
    for k in range(1, hops + 1):
        @pl.when(level - k >= 0)
        def _():
            def pair(shards):
                def run(c, carry):
                    absorb(k, c, shards, False)
                    return carry

                lax.fori_loop(0, kv_heads, run, 0)

            if k < hops:
                await_share(k)
                for c in range(kv_heads):
                    if c == kv_heads - 1 and k >= 1:
                        relay(k + 2)
                    absorb(k, c, (0, 1), False)
            else:
                pair((parity,))
                await_share(k)
                pair((1 - parity,))

    def finish(index, carry):
        total = jnp.sum(part[index], axis=1, keepdims=True)
        result = (acc[index] * (1.0 / total)).astype(out_ref.dtype)
        out_ref[:, pl.ds(pl.multiple_of(index * HD, HD), HD)] = result
        return carry

    lax.fori_loop(0, kv_heads * GROUPS, finish, 0, unroll=2)

    for d in range(1, head_len):
        for which in range(2):
            kv_piece(d, which, sources[which]).wait_send()
        for c in range(kv_heads):
            q_piece(d, c).wait_send()
    for which in range(2):
        share(0, which).wait_send()
        for k in range(1, hops + 1):
            @pl.when(level + k < levels)
            def _():
                push(k, which).wait_send()

            @pl.when(level - k >= 0)
            def _():
                share(k, which).wait_send()


def body(queries, keys, values, doc_ids):
    tok_len, head_len = lax.axis_size("tok"), lax.axis_size("head")
    shard = queries.shape[0] * head_len
    kv_heads = KVH // head_len
    wide = GROUPS * HD
    hops = min((REACH + 1) // 2, tok_len // 2 - 1)
    heads = kv_heads * GROUPS
    DMA = pltpu.SemaphoreType.DMA
    anywhere = pl.BlockSpec(memory_space=pl.ANY)
    vmem = pl.BlockSpec(memory_space=pltpu.VMEM)
    return pl.pallas_call(
        functools.partial(kernel, tok_len, head_len, hops),
        out_shape=jax.ShapeDtypeStruct((shard, heads * HD), jnp.bfloat16),
        in_specs=[anywhere, anywhere, anywhere, vmem],
        out_specs=vmem,
        scratch_shapes=[
            pltpu.VMEM((kv_heads, shard, wide), jnp.bfloat16),
            pltpu.VMEM((hops + 1, 2, 2, shard, kv_heads * HD), jnp.bfloat16),
            pltpu.VMEM((hops + 1, shard, 2 * shard), jnp.float32),
            pltpu.VMEM((heads, shard, HD), jnp.float32),
            pltpu.VMEM((heads, shard, HD), jnp.float32),
            pltpu.VMEM((heads, shard, HD), jnp.float32),
            DMA((2 + kv_heads,)),
            DMA((head_len, 2)),
            DMA((head_len, 2)),
            DMA((head_len, kv_heads)),
            DMA((head_len, kv_heads)),
            DMA((hops + 1, 2)),
            DMA((hops + 1, 2)),
            DMA((hops + 1, 2)),
            DMA((hops + 1, 2)),
        ],
        compiler_params=pltpu.CompilerParams(
            collective_id=0, has_side_effects=True, vmem_limit_bytes=64 * 1000 * 1000
        ),
    )(queries, keys, values, doc_ids.reshape(1, -1))


def solution(mesh):
    return jax.shard_map(
        body,
        mesh=mesh,
        in_specs=(
            P(("tok", "head"), None),
            P(("tok", "head"), None),
            P(("tok", "head"), None),
            P(),
        ),
        out_specs=P("tok", "head"),
        check_vma=False,
    )
```

```python
import functools

import jax
import jax.numpy as jnp
from jax import lax
from jax.experimental import pallas as pl
from jax.experimental.pallas import tpu as pltpu
from jax.sharding import PartitionSpec as P

QH = 64
KVH = 8
HD = 128
REACH = 7
GROUPS = QH // KVH
MESH = pl.DeviceIdType.MESH
NEG = -1e30
SCALE = HD ** -0.5 * 1.4426950408889634
PAIR = 8


def kernel(
    tok_len, head_len, hops,
    q_hbm, k_hbm, v_hbm, ids_ref, out_ref,
    q_buf, kv, bias, peak, part, acc,
    own_sem, kv_send, kv_recv, q_send, q_recv, z_send, z_recv, x_send, x_recv,
):
    t, h = lax.axis_index("tok"), lax.axis_index("head")
    level, parity = t // 2, lax.rem(t, 2)
    partner = level * 2 + (1 - parity)
    levels = tok_len // 2
    piece = q_hbm.shape[0]
    kv_heads, shard, wide = q_buf.shape
    q_cols, kv_cols = kv_heads * wide, kv_heads * HD

    barrier = pltpu.get_barrier_semaphore()
    greeted = head_len
    for d in range(1, head_len):
        pl.semaphore_signal(
            barrier, inc=1, device_id={"tok": t, "head": lax.rem(h + d, head_len)}, device_id_type=MESH
        )
    pl.semaphore_signal(barrier, inc=1, device_id={"tok": partner, "head": h}, device_id_type=MESH)
    for k in range(1, hops + 1):
        @pl.when(level + k < levels)
        def _():
            pl.semaphore_signal(barrier, inc=1, device_id={"tok": t + 2 * k, "head": h}, device_id_type=MESH)

        @pl.when(level - k >= 0)
        def _():
            pl.semaphore_signal(barrier, inc=1, device_id={"tok": t - 2 * k, "head": h}, device_id_type=MESH)
    greeted = greeted + jnp.minimum(levels - 1 - level, hops) + jnp.minimum(level, hops)
    pl.semaphore_wait(barrier, greeted)

    rows = pl.ds(pl.multiple_of(h * piece, piece), piece)

    def kv_piece(d, which, source):
        g = lax.rem(h + d, head_len)
        return pltpu.make_async_remote_copy(
            src_ref=source.at[:, pl.ds(pl.multiple_of(g * kv_cols, kv_cols), kv_cols)],
            dst_ref=kv.at[0, parity, which, rows, :],
            send_sem=kv_send.at[d, which],
            recv_sem=kv_recv.at[d, which],
            device_id={"tok": t, "head": g},
            device_id_type=MESH,
        )

    def q_piece(d, c):
        g = lax.rem(h + d, head_len)
        return pltpu.make_async_remote_copy(
            src_ref=q_hbm.at[:, pl.ds(pl.multiple_of(g * q_cols + c * wide, wide), wide)],
            dst_ref=q_buf.at[c, rows, :],
            send_sem=q_send.at[d, c],
            recv_sem=q_recv.at[d, c],
            device_id={"tok": t, "head": g},
            device_id_type=MESH,
        )

    def own_kv(which, source):
        return pltpu.make_async_copy(
            source.at[:, pl.ds(pl.multiple_of(h * kv_cols, kv_cols), kv_cols)],
            kv.at[0, parity, which, rows, :],
            own_sem.at[which],
        )

    def own_q(c):
        return pltpu.make_async_copy(
            q_hbm.at[:, pl.ds(pl.multiple_of(h * q_cols + c * wide, wide), wide)],
            q_buf.at[c, rows, :],
            own_sem.at[2 + c],
        )

    def push(k, which):
        return pltpu.make_async_remote_copy(
            src_ref=kv.at[0, parity, which],
            dst_ref=kv.at[k, parity, which],
            send_sem=z_send.at[k, which],
            recv_sem=z_recv.at[k, which],
            device_id={"tok": t + 2 * k, "head": h},
            device_id_type=MESH,
        )

    def share(k, which):
        return pltpu.make_async_remote_copy(
            src_ref=kv.at[k, parity, which],
            dst_ref=kv.at[k, parity, which],
            send_sem=x_send.at[k, which],
            recv_sem=x_recv.at[k, which],
            device_id={"tok": partner, "head": h},
            device_id_type=MESH,
        )

    sources = (k_hbm, v_hbm)
    for d in range(1, head_len):
        for which in range(2):
            kv_piece(d, which, sources[which]).start()
    for which in range(2):
        own_kv(which, sources[which]).start()
    for which in range(2):
        own_kv(which, sources[which]).wait()
        for d in range(1, head_len):
            kv_piece(d, which, sources[which]).wait_recv()
        share(0, which).start()
        for k in range(1, 2):
            @pl.when(level + k < levels)
            def _():
                push(k, which).start()
    for k in range(2, hops + 1):
        @pl.when(level + k < levels)
        def _():
            for which in range(2):
                push(k, which).start()
    for c in range(kv_heads):
        for d in range(1, head_len):
            q_piece(d, c).start()
        own_q(c).start()

    own_ids = ids_ref[:, pl.ds(pl.multiple_of(t * shard, shard), shard)]
    column = jnp.broadcast_to(own_ids, (2 * shard, shard)).T
    q_pos = t * shard + lax.broadcasted_iota(jnp.int32, (shard, 2 * shard), 0)
    k_iota = lax.broadcasted_iota(jnp.int32, (shard, 2 * shard), 1)
    for k in range(hops + 1):
        @pl.when(level - k >= 0)
        def _():
            start = (level - k) * 2 * shard
            key_ids = ids_ref[:, pl.ds(pl.multiple_of(start, 2 * shard), 2 * shard)]
            visible = (column == key_ids) & (start + k_iota <= q_pos)
            bias[k] = jnp.where(visible, 0.0, NEG)

    def absorb(k, c, shards, first):
        heads = pl.ds(pl.multiple_of(c * HD, HD), HD)

        def stack(j, carry):
            index = c * GROUPS + j * PAIR
            keys = jnp.concatenate([kv[k, s, 0, :, heads] for s in shards], axis=0)
            vals = jnp.concatenate([kv[k, s, 1, :, heads] for s in shards], axis=0)
            q = jnp.concatenate([
                q_buf[c, :, pl.ds(pl.multiple_of((j * PAIR + i) * HD, HD), HD)] for i in range(PAIR)
            ], axis=0)
            scores = lax.dot_general(
                q, keys, (((1,), (1,)), ((), ())), preferred_element_type=jnp.float32
            )
            rounded, decays = [], []
            for i in range(PAIR):
                tiles = []
                for n, s in enumerate(shards):
                    part_scores = scores[i * shard:(i + 1) * shard, n * shard:(n + 1) * shard]
                    part_scores = part_scores * SCALE + bias[k, :, pl.ds(pl.multiple_of(s * shard, shard), shard)]
                    tiles += [part_scores[:, x:x + HD] for x in range(0, shard, HD)]
                top = functools.reduce(jnp.maximum, tiles)
                top = jnp.broadcast_to(jnp.max(top, axis=1, keepdims=True), (shard, HD))
                if not first:
                    before = peak[index + i]
                    top = jnp.maximum(before, top)
                    decays.append(jnp.exp2(before - top))
                peak[index + i] = top
                weights = [jnp.exp2(tile - top) for tile in tiles]
                total = functools.reduce(jnp.add, weights)
                if not first:
                    total = part[index + i] * decays[i] + total
                part[index + i] = total
                rounded.append(jnp.concatenate([w.astype(jnp.bfloat16) for w in weights], axis=1))
            update = jnp.dot(jnp.concatenate(rounded, axis=0), vals, preferred_element_type=jnp.float32)
            for i in range(PAIR):
                mine = update[i * shard:(i + 1) * shard]
                if not first:
                    mine = acc[index + i] * decays[i] + mine
                acc[index + i] = mine
            return carry

        lax.fori_loop(0, GROUPS // PAIR, stack, 0)

    def relay(k):
        if k <= hops:
            @pl.when(level - k >= 0)
            def _():
                for which in range(2):
                    push(k, which).wait_recv()
                    share(k, which).start()

    def await_share(k):
        for which in range(2):
            share(k, which).wait_recv()

    relay(1)
    await_share(0)
    for c in range(kv_heads):
        own_q(c).wait()
        for d in range(1, head_len):
            q_piece(d, c).wait_recv()
        if c == kv_heads - 1:
            relay(2)
        absorb(0, c, (0, 1), True)
    for k in range(1, hops + 1):
        @pl.when(level - k >= 0)
        def _():
            def pair(shards):
                def run(c, carry):
                    absorb(k, c, shards, False)
                    return carry

                lax.fori_loop(0, kv_heads, run, 0)

            if k < hops:
                await_share(k)
                for c in range(kv_heads):
                    if c == kv_heads - 1 and k >= 1:
                        relay(k + 2)
                    absorb(k, c, (0, 1), False)
            else:
                pair((parity,))
                await_share(k)
                pair((1 - parity,))

    def finish(index, carry):
        total = jnp.sum(part[index], axis=1, keepdims=True)
        result = (acc[index] * (1.0 / total)).astype(out_ref.dtype)
        out_ref[:, pl.ds(pl.multiple_of(index * HD, HD), HD)] = result
        return carry

    lax.fori_loop(0, kv_heads * GROUPS, finish, 0, unroll=2)

    for d in range(1, head_len):
        for which in range(2):
            kv_piece(d, which, sources[which]).wait_send()
        for c in range(kv_heads):
            q_piece(d, c).wait_send()
    for which in range(2):
        share(0, which).wait_send()
        for k in range(1, hops + 1):
            @pl.when(level + k < levels)
            def _():
                push(k, which).wait_send()

            @pl.when(level - k >= 0)
            def _():
                share(k, which).wait_send()


def body(queries, keys, values, doc_ids):
    tok_len, head_len = lax.axis_size("tok"), lax.axis_size("head")
    shard = queries.shape[0] * head_len
    kv_heads = KVH // head_len
    wide = GROUPS * HD
    hops = min((REACH + 1) // 2, tok_len // 2 - 1)
    heads = kv_heads * GROUPS
    DMA = pltpu.SemaphoreType.DMA
    anywhere = pl.BlockSpec(memory_space=pl.ANY)
    vmem = pl.BlockSpec(memory_space=pltpu.VMEM)
    return pl.pallas_call(
        functools.partial(kernel, tok_len, head_len, hops),
        out_shape=jax.ShapeDtypeStruct((shard, heads * HD), jnp.bfloat16),
        in_specs=[anywhere, anywhere, anywhere, vmem],
        out_specs=vmem,
        scratch_shapes=[
            pltpu.VMEM((kv_heads, shard, wide), jnp.bfloat16),
            pltpu.VMEM((hops + 1, 2, 2, shard, kv_heads * HD), jnp.bfloat16),
            pltpu.VMEM((hops + 1, shard, 2 * shard), jnp.float32),
            pltpu.VMEM((heads, shard, HD), jnp.float32),
            pltpu.VMEM((heads, shard, HD), jnp.float32),
            pltpu.VMEM((heads, shard, HD), jnp.float32),
            DMA((2 + kv_heads,)),
            DMA((head_len, 2)),
            DMA((head_len, 2)),
            DMA((head_len, kv_heads)),
            DMA((head_len, kv_heads)),
            DMA((hops + 1, 2)),
            DMA((hops + 1, 2)),
            DMA((hops + 1, 2)),
            DMA((hops + 1, 2)),
        ],
        compiler_params=pltpu.CompilerParams(
            collective_id=0, has_side_effects=True, vmem_limit_bytes=64 * 1000 * 1000
        ),
    )(queries, keys, values, doc_ids.reshape(1, -1))


def solution(mesh):
    return jax.shard_map(
        body,
        mesh=mesh,
        in_specs=(
            P(("tok", "head"), None),
            P(("tok", "head"), None),
            P(("tok", "head"), None),
            P(),
        ),
        out_specs=P("tok", "head"),
        check_vma=False,
    )
```
